32 devices in a mesh: dp: 8 (over y, x, core), tensor: 4 (over z).
Axes of the slice: x: 2, y: 2, z: 4, core: 2. Of those that a mesh axis runs over, the one named last changes fastest.
Arguments:
- hidden_in: bfloat16 [16384, 1024], P(('dp', 'tensor')), may hold values from -6 to 6
- out_grad: bfloat16 [16384, 1024], P(('dp', 'tensor')), may hold values from -6 to 6
- attn_weight: bfloat16 [4, 1024, 1024], P(None, 'dp', 'tensor'), may hold values from -2 to 2
- mlp_weight: bfloat16 [3, 1024, 2624], P(None, 'dp', 'tensor'), may hold values from -2 to 2
- norm_gain: bfloat16 [2, 1024], replicated, may hold values from 0.5 to 1.5
- attn_first: float32 [4, 1024, 1024], P(None, 'dp', 'tensor'), may hold values from -60 to 60
- attn_second: float32 [4, 1024, 1024], P(None, 'dp', 'tensor'), may hold values from 100 to 3000
- attn_left: float32 [4, 1024, 512], P(None, 'dp', 'tensor'), may hold values from -2 to 3
- attn_right: float32 [4, 2048, 1024], P(None, 'dp', 'tensor'), may hold values from -2 to 3
- mlp_first: float32 [3, 1024, 2624], P(None, 'dp', 'tensor'), may hold values from -60 to 60
- mlp_second: float32 [3, 1024, 2624], P(None, 'dp', 'tensor'), may hold values from 100 to 3000
- mlp_left: float32 [3, 1024, 512], P(None, 'dp', 'tensor'), may hold values from -2 to 3
- mlp_right: float32 [3, 5248, 2624], P(None, 'dp', 'tensor'), may hold values from -2 to 3
- gain_first: float32 [2, 1024], replicated, may hold values from -60 to 60
- gain_second: float32 [2, 1024], replicated, may hold values from 100 to 3000
- owner_rows: int32 [8], replicated, may hold values from 0 to 7, each once
- segment_ids: int32 [16384], P('dp'), may hold values from 0 to 15, as said below
- positions: int32 [16384], P('dp'), may hold values from 0 to 1023, as said below
- valid: int32 [16384], P('dp'), may hold values from 0 to 1, as said below
- step: int32 [], replicated, may hold values from 1 to 20
- learn_rate: float32 [], replicated, may hold values from 0.03 to 0.08
- beta_first: float32 [], replicated, may hold values from 0.8 to 0.95
- beta_second: float32 [], replicated, may hold values from 0.9 to 0.99
Outputs:
- output: bfloat16 [16384, 1024], P(('dp', 'tensor'))
- input_grad: bfloat16 [16384, 1024], P(('dp', 'tensor'))
- attn_grad: float32 [4, 1024, 1024], P(None, 'dp', 'tensor')
- mlp_grad: float32 [3, 1024, 2624], P(None, 'dp', 'tensor')
- gain_grad: float32 [2, 1024], replicated
- attn_first_new: float32 [4, 1024, 1024], P(None, 'dp', 'tensor')
- attn_second_new: float32 [4, 1024, 1024], P(None, 'dp', 'tensor')
- mlp_first_new: float32 [3, 1024, 2624], P(None, 'dp', 'tensor')
- mlp_second_new: float32 [3, 1024, 2624], P(None, 'dp', 'tensor')
- gain_first_new: float32 [2, 1024], replicated
- gain_second_new: float32 [2, 1024], replicated
- attn_update: float32 [4, 1024, 1024], P(None, 'dp', 'tensor')
- mlp_update: float32 [3, 1024, 2624], P(None, 'dp', 'tensor')
- gain_update: float32 [2, 1024], replicated
- norm_scale: float32 [7, 8, 4], P(None, 'dp', 'tensor')
- root_means: float32 [4], replicated
The draws below stay inside these ranges and needn't reach their ends.
Inputs may be any that keep to these rules, and one draw needn't show every extreme that they name: `owner_rows`: each index of dp owns a different row block of 128 rows. `segment_ids`: ids restart at 0 with every sequence of 1024 tokens and never fall within it; every document but the last of a sequence has 64 tokens or more. `positions`: 0 at the start of every sequence and wherever segment_ids changes, else one more than the token before. `valid`: within each sequence: 1 on a leading run of at least half of its tokens, 0 after it.
All inputs are finite; a program needn't handle non-finite values.
Results may differ from the reference program's by a relative error of at most 0.014.
Values may be sent and summed in bfloat16 or wider, within the bound.
No kernel may reach another device: no remote copies, remote signals or barrier semaphores. Data moves between devices by JAX's collectives and lax.ppermute only.
A program may use at most 256 MiB of HBM per device.

```python
import math
import jax
import jax.numpy as jnp
from jax import lax

D = 1024
HEADS = 16
HEAD_DIM = 64
FF = 2624
SEQ_LEN = 1024
TOK_GROUP = 2048
TOKENS = 16384
SLAB = 128
ATT_COLS = 256
HID_COLS = 656
BASIS_COLS = 512
ATT_BASIS_ROWS = 2048
HID_BASIS_ROWS = 5248
N_DP = 8
N_TENSOR = 4


def doc_layout(key):
    base_key = jax.random.fold_in(key, 11)
    shortest = max(SEQ_LEN // 16, 1)
    doc_count = SEQ_LEN // shortest
    seq_count = TOKENS // SEQ_LEN
    ticket = jax.random.randint(base_key, (seq_count, doc_count), 1, 4097)
    lengths = jnp.minimum(shortest * (4096 // ticket), SEQ_LEN)
    seq_index = jnp.arange(seq_count, dtype=jnp.int32)[:, None]
    lengths = jnp.where(seq_index == 0, shortest, lengths)
    lengths = jnp.where(seq_index == 1, SEQ_LEN, lengths)
    ends = jnp.cumsum(lengths, axis=1)
    location = jnp.arange(SEQ_LEN, dtype=jnp.int32)
    passed = ends[:, None, :] <= location[None, :, None]
    seg_ids = jnp.sum(passed.astype(jnp.int32), axis=2)
    starts = jnp.max(jnp.where(passed, ends[:, None, :], 0), axis=2)
    return (seg_ids.reshape(TOKENS).astype(jnp.int32), (location[None, :] - starts).reshape(TOKENS).astype(jnp.int32))


def draw_segment_ids(key, part):
    return doc_layout(key)[0]


def draw_positions(key, part):
    return doc_layout(key)[1]


def draw_valid(key, part):
    seq_count = TOKENS // SEQ_LEN
    lengths = jax.random.randint(jax.random.fold_in(key, 23), (seq_count, 1), SEQ_LEN // 2, SEQ_LEN + 1)
    location = jnp.arange(SEQ_LEN, dtype=jnp.int32)[None, :]
    return (location < lengths).astype(jnp.int32).reshape(TOKENS)


def draw_attn_weight(key, part):
    noise = jnp.clip(jax.random.normal(jax.random.fold_in(key, 31), (4, D, D), jnp.float32), -4.0, 4.0)
    factor = jnp.array([1.0, 1.0, 1.0, 4.0], jnp.float32)[:, None, None] * D ** (-0.5)
    return (noise * factor).astype(jnp.bfloat16)


def draw_mlp_weight(key, part):
    noise = jnp.clip(jax.random.normal(jax.random.fold_in(key, 37), (3, D, FF), jnp.float32), -4.0, 4.0)
    factor = jnp.array([D ** (-0.5), D ** (-0.5), 2.0 * FF ** (-0.5)], jnp.float32)[:, None, None]
    return (noise * factor).astype(jnp.bfloat16)


def basis(key, kind_count, row_total, col_total, block_size):
    row_ids = jnp.arange(row_total)[:, None] % block_size
    col_ids = jnp.arange(col_total)[None, :] % block_size
    diagonal = (row_ids == col_ids).astype(jnp.float32)
    noise = jnp.clip(jax.random.normal(key, (kind_count, row_total, col_total), jnp.float32), -4.0, 4.0)
    return diagonal[None] + noise * (0.4 * block_size ** (-0.5))


def draw_attn_left(key, part):
    return basis(jax.random.fold_in(key, 41), 4, D, BASIS_COLS, SLAB)


def draw_attn_right(key, part):
    return basis(jax.random.fold_in(key, 43), 4, ATT_BASIS_ROWS, D, ATT_COLS)


def draw_mlp_left(key, part):
    return basis(jax.random.fold_in(key, 47), 3, D, BASIS_COLS, SLAB)


def draw_mlp_right(key, part):
    return basis(jax.random.fold_in(key, 53), 3, HID_BASIS_ROWS, FF, HID_COLS)


def levels(own_key, extent, shards, least, high):
    def one(dim, parts):
        steps = jax.random.uniform(jax.random.fold_in(jax.random.fold_in(own_key, 6), dim), (parts,), jnp.float32, least / len(shards), high / len(shards))
        return jnp.repeat(jnp.exp(steps), extent[dim] // parts).reshape((-1,) + (1,) * (len(extent) - dim - 1))

    level = one(*shards[0])
    for cut in shards[1:]:
        level = level * one(*cut)
    return level


def bell_draw(own_key, dims, scale, most, cuts=(), kind=jnp.bfloat16):
    loudness = levels(own_key, dims, cuts, -0.22, 0.18) if cuts else 1.0
    drawn = jax.random.normal(own_key, dims, jnp.float32) * scale * loudness
    return jnp.minimum(jnp.maximum(drawn, -most), most).astype(kind)


def setup_inputs(seed: int = 0) -> dict:
    key_list = jax.random.split(jax.random.key(seed), 24)
    return {
        "hidden_in": bell_draw(key_list[0], (TOKENS, D), 1.0, 6.0, ((0, 32),)),
        "out_grad": bell_draw(key_list[1], (TOKENS, D), 1.0, 6.0, ((0, 32),)),
        "attn_weight": draw_attn_weight(jax.random.fold_in(key_list[23], 71), 0),
        "mlp_weight": draw_mlp_weight(jax.random.fold_in(key_list[23], 71), 0),
        "norm_gain": jnp.clip(1.0 + 0.1 * jax.random.normal(key_list[4], (2, D), jnp.float32), 0.5, 1.5).astype(jnp.bfloat16),
        "attn_first": bell_draw(key_list[5], (4, D, D), 10.0, 60.0, ((1, 8), (2, 4)), jnp.float32),
        "attn_second": jnp.clip(jnp.exp(math.log(3000.0) - 3.4011974 * jax.random.uniform(key_list[6], (4, D, D), jnp.float32) ** levels(key_list[6], (4, D, D), ((1, 8), (2, 4)), -0.2, 0.2)), 100.0, 3000.0),
        "attn_left": draw_attn_left(jax.random.fold_in(key_list[23], 71), 0),
        "attn_right": draw_attn_right(jax.random.fold_in(key_list[23], 71), 0),
        "mlp_first": bell_draw(key_list[9], (3, D, FF), 10.0, 60.0, ((1, 8), (2, 4)), jnp.float32),
        "mlp_second": jnp.clip(jnp.exp(math.log(3000.0) - 3.4011974 * jax.random.uniform(key_list[10], (3, D, FF), jnp.float32) ** levels(key_list[10], (3, D, FF), ((1, 8), (2, 4)), -0.2, 0.2)), 100.0, 3000.0),
        "mlp_left": draw_mlp_left(jax.random.fold_in(key_list[23], 71), 0),
        "mlp_right": draw_mlp_right(jax.random.fold_in(key_list[23], 71), 0),
        "gain_first": bell_draw(key_list[13], (2, D), 10.0, 60.0, (), jnp.float32),
        "gain_second": jnp.clip(jnp.exp(jax.random.uniform(key_list[14], (2, D), jnp.float32, math.log(100.0), math.log(3000.0))), 100.0, 3000.0),
        "owner_rows": jax.random.permutation(key_list[15], N_DP).astype(jnp.int32),
        "segment_ids": draw_segment_ids(jax.random.fold_in(key_list[23], 71), 0),
        "positions": draw_positions(jax.random.fold_in(key_list[23], 71), 0),
        "valid": draw_valid(jax.random.fold_in(key_list[23], 71), 0),
        "step": jax.random.randint(key_list[19], (), 1, 21).astype(jnp.int32),
        "learn_rate": jnp.clip(jax.random.uniform(key_list[20], (), jnp.float32, 0.03, 0.08), 0.03, 0.08),
        "beta_first": jnp.clip(jax.random.uniform(key_list[21], (), jnp.float32, 0.8, 0.95), 0.8, 0.95),
        "beta_second": jnp.clip(jax.random.uniform(key_list[22], (), jnp.float32, 0.9, 0.99), 0.9, 0.99),
    }


NORM_EPS = 1e-05
ROPE_BASE = 160000.0
ADAM_EPS = 1e-08
SCALE_EPS = 1e-06
MASKED = -1e+30
PRECISE = lax.Precision.HIGHEST

@jax.custom_vjp
def low(v):
    return lax.optimization_barrier(v.astype(jnp.bfloat16)).astype(jnp.float32)

@jax.custom_vjp
def low_back(v):
    return v

def low_keep(v):
    return (low(v), None)

def low_pass(kept, grad):
    return (grad,)

def back_keep(v):
    return (v, None)

def back_low(kept, grad):
    return (low(grad),)
low.defvjp(low_keep, low_pass)
low_back.defvjp(back_keep, back_low)

def layer_norm(values, gain_row):
    average = lax.optimization_barrier(jnp.mean(values, axis=-1, keepdims=True))
    centred = values - average
    spread = lax.optimization_barrier(jnp.mean(centred * centred, axis=-1, keepdims=True))
    return centred * lax.rsqrt(spread + NORM_EPS) * gain_row

def rope_tables(positions):
    half_dim = HEAD_DIM // 2
    frequency = jnp.exp(jnp.arange(half_dim, dtype=jnp.float32) * (-2.0 * math.log(ROPE_BASE) / HEAD_DIM))
    angles = positions.astype(jnp.float32)[:, None] * frequency[None, :]
    return (jnp.cos(angles)[:, None, :], jnp.sin(angles)[:, None, :])

def rotate(values, cos_table, sin_table):
    half_dim = values.shape[-1] // 2
    lower_half = values[..., :half_dim]
    upper_half = values[..., half_dim:]
    return jnp.concatenate([lower_half * cos_table - upper_half * sin_table, upper_half * cos_table + lower_half * sin_table], axis=-1)

def attend(pieces):
    queries, key_rows, value_rows, seg_row, keep_row = pieces
    location = jnp.arange(seg_row.shape[0])
    allowed = (seg_row[:, None] == seg_row[None, :]) & ((keep_row[None, :] > 0) | (location[:, None] == location[None, :]))
    raw = low_back(jnp.einsum('qhe,khe->hqk', queries, key_rows, precision=PRECISE))
    scores = jnp.where(allowed[None], raw * (1.0 / math.sqrt(HEAD_DIM)), MASKED)
    weights = low(jax.nn.softmax(scores, axis=-1))
    return jnp.einsum('hqk,khe->qhe', weights, value_rows, precision=PRECISE)

def forward(hidden_rows, qkv_weight, out_weight, gate_up_weight, down_weight, gain_rows, seg_rows, pos_rows, keep_rows):
    tokens = hidden_rows.shape[0]
    normed = low(layer_norm(hidden_rows, gain_rows[0]))
    projected = jnp.einsum('td,kdc->ktc', normed, qkv_weight, precision=PRECISE)
    cos_table, sin_table = rope_tables(pos_rows)
    head_shape = (tokens, HEADS, HEAD_DIM)
    queries = low(rotate(low_back(projected[0]).reshape(head_shape), cos_table, sin_table))
    key_rows = low(rotate(low_back(projected[1]).reshape(head_shape), cos_table, sin_table))
    value_rows = low(low_back(projected[2])).reshape(head_shape)
    seq_shape = (tokens // SEQ_LEN, SEQ_LEN, HEADS, HEAD_DIM)
    attended = lax.map(jax.checkpoint(attend), (queries.reshape(seq_shape), key_rows.reshape(seq_shape), value_rows.reshape(seq_shape), seg_rows.reshape(-1, SEQ_LEN), keep_rows.reshape(-1, SEQ_LEN)))
    mixture = low(low_back(attended.reshape(tokens, D)))
    attn_branch = low_back(jnp.einsum('tc,dc->td', mixture, out_weight, precision=PRECISE))
    resid = hidden_rows + attn_branch
    second = low(layer_norm(resid, gain_rows[1]))
    gate_up = jnp.einsum('td,kdf->ktf', second, gate_up_weight, precision=PRECISE)
    activated = low(jax.nn.gelu(low_back(gate_up[0]), approximate=False) * low_back(gate_up[1]))
    mlp_branch = low_back(jnp.einsum('tf,df->td', activated, down_weight, precision=PRECISE))
    return (resid + mlp_branch, (attn_branch, resid, mlp_branch))

def to_model(stored, owner_rows):
    kind_count, row_total, col_total = stored.shape
    blocks = stored.reshape(kind_count, N_DP, SLAB, col_total)
    return jnp.zeros_like(blocks).at[:, owner_rows].set(blocks).reshape(kind_count, row_total, col_total)

def to_owner(model, owner_rows):
    kind_count, row_total, col_total = model.shape
    return model.reshape(kind_count, N_DP, SLAB, col_total)[:, owner_rows].reshape(kind_count, row_total, col_total)

def soap_step(grad_full, first, second, left, right, width, step_size, beta_one, beta_two):
    kind_count = grad_full.shape[0]
    grad_five = grad_full.reshape(kind_count, N_DP, SLAB, N_TENSOR, width)
    left_five = left.reshape(kind_count, N_DP, SLAB, N_TENSOR, SLAB)
    right_five = right.reshape(kind_count, N_DP, width, N_TENSOR, width)
    half_turn = jnp.einsum('kiajb,kiajc->kibjc', left_five, grad_five, precision=PRECISE)
    rotated = jnp.einsum('kibjc,kicje->kibje', half_turn, right_five, precision=PRECISE).reshape(grad_full.shape)
    first_new = beta_one * first + (1.0 - beta_one) * rotated
    second_new = beta_two * second + (1.0 - beta_two) * rotated * rotated
    direction = first_new / (jnp.sqrt(second_new) + ADAM_EPS)
    dir_five = direction.reshape(kind_count, N_DP, SLAB, N_TENSOR, width)
    back_half = jnp.einsum('kiajb,kibje->kiaje', left_five, dir_five, precision=PRECISE)
    turned = jnp.einsum('kiaje,kicje->kiajc', back_half, right_five, precision=PRECISE)
    factor = jnp.sqrt(lax.optimization_barrier(jnp.mean(dir_five * dir_five, axis=(2, 4)))) * lax.rsqrt(lax.optimization_barrier(jnp.mean(turned * turned, axis=(2, 4))) + SCALE_EPS)
    update = -step_size * factor[:, :, None, :, None] * turned
    return (first_new, second_new, update.reshape(grad_full.shape), factor)

def reference(hidden_in, out_grad, attn_weight, mlp_weight, norm_gain, attn_first, attn_second, attn_left, attn_right, mlp_first, mlp_second, mlp_left, mlp_right, gain_first, gain_second, owner_rows, segment_ids, positions, valid, step, learn_rate, beta_first, beta_second):
    attn_model = to_model(attn_weight.astype(jnp.float32), owner_rows)
    mlp_model = to_model(mlp_weight.astype(jnp.float32), owner_rows)
    gain_rows = norm_gain.astype(jnp.float32)

    def one_group(totals, pieces):
        rows_in, grad_rows, seg_rows, pos_rows, keep_rows = pieces

        def run_layer(hidden_rows, qkv_weight, out_weight, gate_up_weight, down_weight, gain_vals):
            return forward(hidden_rows, qkv_weight, out_weight, gate_up_weight, down_weight, gain_vals, seg_rows, pos_rows, keep_rows)
        result, pullback, extras = jax.vjp(run_layer, rows_in.astype(jnp.float32), attn_model[:3], attn_model[3], mlp_model[:2], mlp_model[2], gain_rows, has_aux=True)
        grads = pullback(grad_rows.astype(jnp.float32))
        attn_branch, resid, mlp_branch = extras
        keep_mask = keep_rows.astype(jnp.float32)[:, None]
        stat_terms = jnp.stack([jnp.sum(keep_mask), jnp.sum(keep_mask * attn_branch * attn_branch), jnp.sum(keep_mask * resid * resid), jnp.sum(keep_mask * mlp_branch * mlp_branch), jnp.sum(keep_mask * result * result)])
        totals = (totals[0] + grads[1], totals[1] + grads[2], totals[2] + grads[3], totals[3] + grads[4], totals[4] + grads[5], totals[5] + stat_terms)
        return (totals, (result.astype(jnp.bfloat16), grads[0].astype(jnp.bfloat16)))
    start_totals = (jnp.zeros((3, D, D), jnp.float32), jnp.zeros((D, D), jnp.float32), jnp.zeros((2, D, FF), jnp.float32), jnp.zeros((D, FF), jnp.float32), jnp.zeros((2, D), jnp.float32), jnp.zeros((5,), jnp.float32))
    sliced = (hidden_in.reshape(N_DP, TOK_GROUP, D), out_grad.reshape(N_DP, TOK_GROUP, D), segment_ids.reshape(N_DP, TOK_GROUP), positions.reshape(N_DP, TOK_GROUP), valid.reshape(N_DP, TOK_GROUP))
    totals, (outputs, input_grads) = lax.scan(one_group, start_totals, sliced)
    attn_grad = to_owner(jnp.concatenate([totals[0], totals[1][None]], axis=0), owner_rows)
    mlp_grad = to_owner(jnp.concatenate([totals[2], totals[3][None]], axis=0), owner_rows)
    gain_grad = totals[4]
    step_count = step.astype(jnp.float32)
    step_size = learn_rate * jnp.sqrt(1.0 - jnp.power(beta_second, step_count)) / (1.0 - jnp.power(beta_first, step_count))
    attn_first_new, attn_second_new, attn_update, attn_scale = soap_step(attn_grad, attn_first, attn_second, attn_left, attn_right, ATT_COLS, step_size, beta_first, beta_second)
    mlp_first_new, mlp_second_new, mlp_update, mlp_scale = soap_step(mlp_grad, mlp_first, mlp_second, mlp_left, mlp_right, HID_COLS, step_size, beta_first, beta_second)
    gain_first_new = beta_first * gain_first + (1.0 - beta_first) * gain_grad
    gain_second_new = beta_second * gain_second + (1.0 - beta_second) * gain_grad * gain_grad
    gain_update = -step_size * gain_first_new / (jnp.sqrt(gain_second_new) + ADAM_EPS)
    stat_sums = totals[5]
    root_means = jnp.sqrt(stat_sums[1:] / (stat_sums[0] * D))
    norm_scale = jnp.concatenate([attn_scale, mlp_scale], axis=0)
    return (outputs.reshape(TOKENS, D), input_grads.reshape(TOKENS, D), attn_grad, mlp_grad, gain_grad, attn_first_new, attn_second_new, mlp_first_new, mlp_second_new, gain_first_new, gain_second_new, attn_update, mlp_update, gain_update, norm_scale, root_means)
```

```python
import functools
import math

import jax
import jax.numpy as jnp
from jax import lax
from jax.experimental import pallas as pl
from jax.experimental.pallas import tpu as pltpu
from jax.sharding import PartitionSpec as P

D = 1024
HEADS = 16
HEAD_DIM = 64
SEQ_LEN = 1024
NORM_EPS = 1e-05
ROPE_BASE = 160000.0
ADAM_EPS = 1e-08
SCALE_EPS = 1e-06
PRECISE = lax.Precision.HIGHEST
F32 = jnp.float32
BF = jnp.bfloat16
AXES = ("dp", "tensor")
TN = (((0,), (0,)), ((), ()))

NT=(((1,),(1,)),((),()))
NN=(((1,),(0,)),((),()))
def dot(a,b,dims=NN):
    return lax.dot_general(a,b,dims,preferred_element_type=F32)

def swap_halves(x):
    lane=lax.broadcasted_iota(jnp.int32,x.shape,1)
    return jnp.where(lane%64<32,pltpu.roll(x,96,1),pltpu.roll(x,32,1))

def fwd_kernel(chunk,qraw,kraw,vraw,cosk,sink,segq,segk,keepk,o_ref,q_ref,k_ref,v_ref,p_ref,r_ref,bias):
    rows_q=qraw.shape[0]; rows_k=kraw.shape[0]
    @pl.when(pl.program_id(0)==0)
    def _():
        ki=lax.broadcasted_iota(jnp.int32,(rows_k,rows_q),0)
        qi=lax.broadcasted_iota(jnp.int32,(rows_k,rows_q),1)
        ok=(segk[...]==segq[...])&((keepk[...]>0)|(ki==qi))
        bias[...]=jnp.where(ok,0.0,-1e30)
    q32=qraw[...]; k32=kraw[...]
    q=(q32*cosk[:rows_q]+swap_halves(q32)*sink[:rows_q]).astype(BF)
    k=(k32*cosk[...]+swap_halves(k32)*sink[...]).astype(BF)
    q_ref[...]=q; k_ref[...]=k
    v32=vraw[...]
    v_ref[...]=v32.astype(BF)
    vt=v32.T.astype(BF)
    lane=lax.broadcasted_iota(jnp.int32,q.shape,1)
    row=lax.broadcasted_iota(jnp.int32,(128,1),0)
    qs=q*jnp.asarray(0.125,BF)
    parts=[]
    qh=[jnp.where(lane//64==h,qs,jnp.zeros_like(qs)) for h in range(2)]
    for c in range(rows_q//chunk):
        sl=slice(c*chunk,(c+1)*chunk)
        outs=[]
        for h in range(2):
            s=dot(k,qh[h][sl],NT)+bias[:,sl]
            m=jnp.max(s,axis=0,keepdims=True)
            p=jnp.exp(s-m)
            l=jnp.sum(p,axis=0,keepdims=True)
            pb=p.astype(BF)
            p_ref[h,:,sl]=pb
            r=1.0/l
            r_ref[0,h:h+1,sl]=r
            outs.append(dot(vt,pb)*r)
        parts.append(jnp.where(row<64,outs[0],outs[1]))
    ot=jnp.concatenate(parts,axis=1) if len(parts)>1 else parts[0]
    o_ref[...]=ot.T.astype(BF)

def attn_fwd(qraw,kraw,vraw,cosk,sink,segq,segk,keepk,chunk=512):
    rq,width=qraw.shape; rk=kraw.shape[0]; pairs=width//128
    chunk=min(chunk,rq)
    sd=jax.ShapeDtypeStruct
    col=lambda r:pl.BlockSpec((r,128),lambda i:(0,i))
    full=lambda a:pl.BlockSpec(a.shape,lambda i:(0,0))
    return pl.pallas_call(functools.partial(fwd_kernel,chunk),grid=(pairs,),
        in_specs=[col(rq),col(rk),col(rk),full(cosk),full(sink),full(segq),full(segk),full(keepk)],
        out_specs=[col(rq),col(rq),col(rk),col(rk),pl.BlockSpec((2,rk,rq),lambda i:(i,0,0)),pl.BlockSpec((1,2,rq),lambda i:(i,0,0))],
        out_shape=[sd((rq,width),BF),sd((rq,width),BF),sd((rk,width),BF),sd((rk,width),BF),sd((2*pairs,rk,rq),BF),sd((pairs,2,rq),F32)],
        scratch_shapes=[pltpu.VMEM((rk,rq),F32)],
        compiler_params=pltpu.CompilerParams(dimension_semantics=("arbitrary",),vmem_limit_bytes=60<<20),
        cost_estimate=pl.CostEstimate(flops=4*rq*rk*width,bytes_accessed=4*pairs*rk*rq+12*rk*width,transcendentals=2*pairs*rk*rq),
        name="attn_fwd")(qraw,kraw,vraw,cosk,sink,segq,segk,keepk)

def bwd_kernel(chunk,q_ref,k_ref,v_ref,o_ref,do_ref,p_ref,r_ref,cosk,sink,dq_ref,dk_ref,dv_ref):
    rows_q=q_ref.shape[0]
    q=q_ref[...]; k=k_ref[...]; v=v_ref[...]
    kt=k.astype(F32).T
    dot_t=do_ref[...].astype(F32).T
    o_t=o_ref[...].astype(F32).T
    row=lax.broadcasted_iota(jnp.int32,(128,1),0)
    lane=lax.broadcasted_iota(jnp.int32,(1,128),1)
    r=r_ref[0]
    dpt=dot_t*jnp.where(row<64,r[0:1],r[1:2])
    dprod=dpt*o_t
    dp_rows=dpt.T
    dk=jnp.zeros(k.shape,F32); dv=jnp.zeros(k.shape,F32)
    dqs=[]
    for c in range(rows_q//chunk):
        sl=slice(c*chunk,(c+1)*chunk)
        dqt=None
        for h in range(2):
            hs=slice(h*64,(h+1)*64)
            p=p_ref[h,:,sl]
            dh=jnp.where(row//64==h,dpt[:,sl],0.0).astype(BF)
            dp=dot(v,dh)
            delta=jnp.sum(dprod[hs,sl],axis=0,keepdims=True)
            ds=(p.astype(F32)*(dp-delta)).astype(BF)
            kh=jnp.where(row//64==h,kt,0.0).astype(BF)
            t=dot(kh,ds)
            dqt=t if dqt is None else dqt+t
            qh=jnp.where(lane//64==h,q[sl],jnp.zeros_like(q[sl]))
            dk=dk+dot(ds,qh)
            dh2=jnp.where(lane//64==h,dp_rows[sl],0.0).astype(BF)
            dv=dv+dot(p,dh2)
        dqs.append(dqt)
    dqt=jnp.concatenate(dqs,axis=1) if len(dqs)>1 else dqs[0]
    dq=dqt.T
    dq=(dq*cosk[:rows_q]-swap_halves(dq)*sink[:rows_q])*0.125
    dk=(dk*cosk[...]-swap_halves(dk)*sink[...])*0.125
    dq_ref[...]=dq.astype(BF); dk_ref[...]=dk.astype(BF); dv_ref[...]=dv.astype(BF)

def attn_bwd(q,k,v,o,do,p,r,cosk,sink,chunk=512):
    rq,width=q.shape; rk=k.shape[0]; pairs=width//128
    chunk=min(chunk,rq)
    sd=jax.ShapeDtypeStruct
    col=lambda n:pl.BlockSpec((n,128),lambda i:(0,i))
    full=lambda a:pl.BlockSpec(a.shape,lambda i:(0,0))
    return pl.pallas_call(functools.partial(bwd_kernel,chunk),grid=(pairs,),
        in_specs=[col(rq),col(rk),col(rk),col(rq),col(rq),pl.BlockSpec((2,rk,rq),lambda i:(i,0,0)),pl.BlockSpec((1,2,rq),lambda i:(i,0,0)),full(cosk),full(sink)],
        out_specs=[col(rq),col(rk),col(rk)],
        out_shape=[sd((rq,width),BF),sd((rk,width),BF),sd((rk,width),BF)],
        compiler_params=pltpu.CompilerParams(dimension_semantics=("arbitrary",),vmem_limit_bytes=60<<20),
        cost_estimate=pl.CostEstimate(flops=8*rq*rk*width,bytes_accessed=4*pairs*rk*rq+12*rk*width,transcendentals=0),
        name="attn_bwd")(q,k,v,o,do,p,r,cosk,sink)


def norm_stats(values):
    average = jnp.mean(values, axis=-1, keepdims=True)
    centred = values - average
    spread = jnp.mean(centred * centred, axis=-1, keepdims=True)
    scale = lax.rsqrt(spread + NORM_EPS)
    return centred * scale, scale


def norm_back(values, gain_row, grads):
    unit, scale = norm_stats(values)
    inner = grads * gain_row
    part = scale * (
        inner
        - jnp.mean(inner, axis=-1, keepdims=True)
        - unit * jnp.mean(inner * unit, axis=-1, keepdims=True)
    )
    return part, jnp.sum(grads * unit, axis=0)


def gather_rows(shards):
    count, rows, slab = shards.shape
    got = lax.all_gather(shards, AXES, axis=0, tiled=False)
    owners, shards_n = lax.axis_size("dp"), lax.axis_size("tensor")
    got = got.reshape(owners, shards_n, count, rows, slab).transpose(2, 1, 3, 0, 4)
    return got.reshape(count, shards_n * rows, owners * slab)


def scatter_rows(grads):
    owners, shards_n = lax.axis_size("dp"), lax.axis_size("tensor")
    stack = jnp.stack([g.astype(BF) for g in grads])
    count, rows, width = stack.shape
    stack = stack.reshape(count, shards_n, rows // shards_n, owners, width // owners)
    stack = stack.transpose(3, 1, 0, 2, 4).reshape(
        owners * shards_n, count, rows // shards_n, width // owners
    )
    out = lax.psum_scatter(stack, AXES, scatter_dimension=0, tiled=True)
    return out[0].astype(F32)


def sum_all(value):
    for axis in AXES:
        size = lax.axis_size(axis)
        bit = 1
        while bit < size:
            value = value + lax.ppermute(value, axis, [(i, i ^ bit) for i in range(size)])
            bit *= 2
    return value


def soap_block(grad_block, first, second, left, right, step_size, beta_one, beta_two):
    half_turn = jnp.einsum("kab,kac->kbc", left, grad_block, precision=PRECISE)
    rotated = jnp.einsum("kbc,kce->kbe", half_turn, right, precision=PRECISE)
    first_new = beta_one * first + (1.0 - beta_one) * rotated
    second_new = beta_two * second + (1.0 - beta_two) * rotated * rotated
    direction = first_new / (jnp.sqrt(second_new) + ADAM_EPS)
    back_half = jnp.einsum("kab,kbe->kae", left, direction, precision=PRECISE)
    turned = jnp.einsum("kae,kce->kac", back_half, right, precision=PRECISE)
    factor = jnp.sqrt(jnp.mean(direction * direction, axis=(1, 2))) * lax.rsqrt(
        jnp.mean(turned * turned, axis=(1, 2)) + SCALE_EPS
    )
    update = -step_size * factor[:, None, None] * turned
    return (first_new, second_new, update, factor)


def per_device(
    hidden_in,
    out_grad,
    attn_weight,
    mlp_weight,
    norm_gain,
    attn_first,
    attn_second,
    attn_left,
    attn_right,
    mlp_first,
    mlp_second,
    mlp_left,
    mlp_right,
    gain_first,
    gain_second,
    owner_rows,
    segment_ids,
    positions,
    valid,
    step,
    learn_rate,
    beta_first,
    beta_second,
):
    owners = lax.axis_size("dp")
    shards = lax.axis_size("tensor")
    rows = hidden_in.shape[0]
    slab = D // owners
    parts = SEQ_LEN // rows
    place = lax.axis_index("tensor")
    part = place % parts
    ahead = [(i, i - i % parts + (i + 1) % parts) for i in range(shards)]
    behind = [(j, i) for i, j in ahead]

    hidden_parts = [hidden_in]
    for _ in range(parts - 1):
        hidden_parts.append(lax.ppermute(hidden_parts[-1], "tensor", ahead))

    def of_sequence(values):
        here = lax.dynamic_index_in_dim(
            values.reshape(-1, parts, rows), place // parts, 0, keepdims=False
        )
        turned = jnp.concatenate([here[::-1], here[::-1]], axis=0)
        return lax.dynamic_slice_in_dim(turned, parts - 1 - part, parts, 0).reshape(SEQ_LEN)

    seg_all, pos_all, keep_all = of_sequence(segment_ids), of_sequence(positions), of_sequence(valid)

    attn_t = attn_weight.transpose(0, 2, 1)
    mlp_t = mlp_weight.transpose(0, 2, 1)
    qkv_t = gather_rows(attn_t[:3])
    out_t = gather_rows(attn_t[3:])[0]
    gate_up_t = gather_rows(mlp_t[:2])
    down_t = gather_rows(mlp_t[2:])[0]

    feature = (owner_rows[:, None] * slab + jnp.arange(slab, dtype=jnp.int32)[None, :]).reshape(D)
    to_place = (jnp.arange(D, dtype=jnp.int32)[:, None] == feature[None, :]).astype(BF)
    gain_rows = jnp.dot(norm_gain, to_place, preferred_element_type=F32)

    hidden_all = dot(jnp.concatenate(hidden_parts, axis=0), to_place)
    hidden_own = hidden_all[:rows]
    grad_own = dot(out_grad, to_place)
    grad_low = grad_own.astype(BF)

    first_all = (norm_stats(hidden_all)[0] * gain_rows[0]).astype(BF)
    first_own = first_all[:rows]
    half = HEAD_DIM // 2
    frequency = jnp.exp(jnp.arange(half, dtype=F32) * (-2.0 * math.log(ROPE_BASE) / HEAD_DIM))
    angles = pos_all.astype(F32)[:, None] * frequency[None, :]
    cosine, sine = jnp.cos(angles), jnp.sin(angles)
    cosine = jnp.tile(cosine, (1, 4))
    sine = jnp.tile(jnp.concatenate([-sine, sine], axis=1), (1, 2))
    attended, queries, key_rows, value_rows, weights, inverse_sums = attn_fwd(
        dot(first_own, qkv_t[0], NT),
        dot(first_all, qkv_t[1], NT),
        dot(first_all, qkv_t[2], NT),
        cosine,
        sine,
        seg_all[None, :rows],
        seg_all[:, None],
        keep_all[:, None],
    )
    attn_branch = dot(attended, out_t)
    resid = hidden_own + attn_branch
    second_norm = (norm_stats(resid)[0] * gain_rows[1]).astype(BF)
    gate = dot(second_norm, gate_up_t[0], NT)
    up = dot(second_norm, gate_up_t[1], NT)
    normal = 0.5 * (1.0 + lax.erf(gate * math.sqrt(0.5)))
    density = jnp.exp(-0.5 * gate * gate) * (1.0 / math.sqrt(2.0 * math.pi))
    gelu = gate * normal
    activated = (gelu * up).astype(BF)
    by_up = gelu.astype(BF)
    by_gate = (up * (normal + gate * density)).astype(BF)
    mlp_branch = dot(activated, down_t)
    result = resid + mlp_branch
    output = dot(result.astype(BF), to_place, NT).astype(BF)
    keep_own = lax.dynamic_slice_in_dim(valid, place * rows, rows, 0).astype(F32)[:, None]
    stat_terms = jnp.stack(
        [
            jnp.sum(keep_own),
            jnp.sum(keep_own * attn_branch * attn_branch),
            jnp.sum(keep_own * resid * resid),
            jnp.sum(keep_own * mlp_branch * mlp_branch),
            jnp.sum(keep_own * result * result),
        ]
    )

    hidden_grad = dot(grad_low, down_t, NT)
    gate_grad = (hidden_grad * by_gate).astype(BF)
    up_grad = (hidden_grad * by_up).astype(BF)
    mlp_grads = scatter_rows(
        [
            dot(gate_grad, second_norm, TN),
            dot(up_grad, second_norm, TN),
            dot(activated, grad_low, TN),
        ]
    )
    second_grad = dot(gate_grad, gate_up_t[0]) + dot(up_grad, gate_up_t[1])
    resid_part, gain_two = norm_back(resid, gain_rows[1], second_grad)
    resid_grad = grad_own + resid_part
    resid_low = resid_grad.astype(BF)
    mixed_grad = dot(resid_low, out_t, NT).astype(BF)
    out_wgrad = dot(attended, resid_low, TN)
    dq, dk, dv = attn_bwd(
        queries, key_rows, value_rows, attended, mixed_grad, weights, inverse_sums, cosine, sine
    )
    attn_grads = scatter_rows(
        [dot(dq, first_own, TN), dot(dk, first_all, TN), dot(dv, first_all, TN), out_wgrad]
    )
    late = dot(dk, qkv_t[1]) + dot(dv, qkv_t[2])
    others = dot(late[rows:].astype(BF), to_place, NT).astype(BF)
    passed = None
    for back in range(parts - 1, 0, -1):
        mine = others[(back - 1) * rows : back * rows]
        if passed is not None:
            mine = (mine.astype(F32) + passed.astype(F32)).astype(BF)
        passed = lax.ppermute(mine, "tensor", behind)
    first_grad = dot(dq, qkv_t[0]) + late[:rows]
    if passed is not None:
        first_grad = first_grad + dot(passed, to_place)
    input_part, gain_one = norm_back(hidden_own, gain_rows[0], first_grad)
    input_grad = dot((resid_grad + input_part).astype(BF), to_place, NT).astype(BF)

    gain_part = lax.dot_general(
        jnp.stack([gain_one, gain_two]),
        to_place.astype(F32),
        NT,
        precision=PRECISE,
        preferred_element_type=F32,
    )
    sums = sum_all(
        jnp.concatenate([gain_part, jnp.pad(stat_terms, (0, D - 5))[None]], axis=0)
    )
    gain_grad, stat_sums = sums[:2], sums[2, :5]

    attn_grad = attn_grads.transpose(0, 2, 1)
    mlp_grad = mlp_grads.transpose(0, 2, 1)
    step_count = step.astype(F32)
    step_size = (
        learn_rate
        * jnp.sqrt(1.0 - jnp.power(beta_second, step_count))
        / (1.0 - jnp.power(beta_first, step_count))
    )
    attn_first_new, attn_second_new, attn_update, attn_scale = soap_block(
        attn_grad, attn_first, attn_second, attn_left, attn_right, step_size, beta_first, beta_second
    )
    mlp_first_new, mlp_second_new, mlp_update, mlp_scale = soap_block(
        mlp_grad, mlp_first, mlp_second, mlp_left, mlp_right, step_size, beta_first, beta_second
    )
    gain_first_new = beta_first * gain_first + (1.0 - beta_first) * gain_grad
    gain_second_new = beta_second * gain_second + (1.0 - beta_second) * gain_grad * gain_grad
    gain_update = -step_size * gain_first_new / (jnp.sqrt(gain_second_new) + ADAM_EPS)
    root_means = jnp.sqrt(stat_sums[1:] / (stat_sums[0] * D))
    norm_scale = jnp.concatenate([attn_scale, mlp_scale], axis=0).reshape(7, 1, 1)
    return (
        output,
        input_grad,
        attn_grad,
        mlp_grad,
        gain_grad,
        attn_first_new,
        attn_second_new,
        mlp_first_new,
        mlp_second_new,
        gain_first_new,
        gain_second_new,
        attn_update,
        mlp_update,
        gain_update,
        norm_scale,
        root_means,
    )


def solution(mesh):
    tokens, matrices, whole, group = P(AXES, None), P(None, "dp", "tensor"), P(), P("dp")
    return jax.shard_map(
        per_device,
        mesh=mesh,
        in_specs=(tokens, tokens, matrices, matrices, whole)
        + (matrices,) * 8
        + (whole,) * 3
        + (group,) * 3
        + (whole,) * 4,
        out_specs=(tokens, tokens, matrices, matrices, whole)
        + (matrices,) * 4
        + (whole,) * 2
        + (matrices,) * 2
        + (whole, matrices, whole),
        check_vma=False,
    )
```
